32 devices in a mesh: groups: 2 (over y), rows: 4 (over z), segment: 2 (over x), chan: 2 (over core).
Axes of the slice: x: 2, y: 2, z: 4, core: 2. Of those that a mesh axis runs over, the one named last changes fastest.
Arguments:
- latent: bfloat16 [8, 8, 160, 384], P(('groups', 'segment'), 'rows'), parts along dimension 0, may hold values from -6 to 6
- cache_mid: bfloat16 [4, 8, 160, 384], P('groups', 'rows'), parts along dimension 0, may hold values from -6 to 6
- cache_low: bfloat16 [4, 16, 320, 192], P('groups', 'rows'), parts along dimension 0, may hold values from -6 to 6
- gain_mid: float32 [384], replicated, may hold values from 0.1 to 1.9
- gain_attn: float32 [384], replicated, may hold values from 0.1 to 1.9
- gain_low: float32 [192], replicated, may hold values from 0.1 to 1.9
- conv_mid: bfloat16 [3, 3, 3, 384, 384], P(None, None, None, None, 'chan'), may hold values from -0.0625 to 0.0625
- attn_qkv: bfloat16 [384, 1152], replicated, may hold values from -4 to 4
- attn_proj: bfloat16 [384, 384], replicated, may hold values from -0.3125 to 0.3125
- conv_up: bfloat16 [3, 3, 384, 192], P(None, None, None, 'chan'), may hold values from -0.109375 to 0.109375
- conv_low: bfloat16 [3, 3, 3, 192, 192], P(None, None, None, None, 'chan'), may hold values from -0.078125 to 0.078125
Outputs:
- decoded: bfloat16 [8, 16, 320, 192], P(('groups', 'segment'), 'rows', None, 'chan'), parts along dimension 0
The draws below stay inside these ranges and needn't reach their ends.
There are 2 independent parts, one for each index of `groups`. The reference program is written for one: setup_inputs(seed, part) draws one part's arguments, and reference() takes and returns one part's arrays. A program takes and returns all parts, laid end to end along the dimension named above; an argument that names none is the same for every part. Nothing has to cross between parts.
All inputs are finite; a program needn't handle non-finite values.
Results may differ from the reference program's by a relative error of at most 0.0071.
Values may be sent and summed in bfloat16 or wider, within the bound.
A program may use at most 128 MiB of HBM per device.

```python
import math
import jax
import jax.numpy as jnp
from jax import lax

C1 = 384
C2 = 192
W = 160
H = 8
F = 4


def draw_attn_qkv(key, part):
    first_key = jax.random.fold_in(jax.random.fold_in(key, 17), 0)
    base = jax.random.normal(first_key, (C1, 3 * C1), jnp.float32) / math.sqrt(C1)
    return base.astype(jnp.bfloat16)


def block_scale(key, dims, pieces, smallest, high):
    factor_of, own = 1.0, jax.random.fold_in(key, 6)
    for axis_at, shards_of in pieces:
        steps = jnp.exp(jax.random.uniform(jax.random.fold_in(own, axis_at), (shards_of,), jnp.float32, smallest / len(pieces), high / len(pieces)))
        factor_of = factor_of * jnp.repeat(steps, dims[axis_at] // shards_of).reshape([-1 if axis == axis_at else 1 for axis in range(len(dims))])
    return factor_of


def noise(stream_key, shape, scale, bound, cuts=(), dtype=jnp.bfloat16):
    entries = jax.random.normal(stream_key, shape, jnp.float32) * scale
    if len(cuts) > 0:
        entries = block_scale(stream_key, shape, cuts, -0.22, 0.18) * entries
    return jnp.clip(entries, min=-bound, max=bound).astype(dtype)


def setup_inputs(seed: int = 0, part: int = 0) -> dict:
    seeds = jax.random.split(jax.random.key(seed), 12)
    part_keys = jax.random.split(jax.random.fold_in(seeds[11], part), 12)
    latent = noise(part_keys[0], (F, H, W, C1), 1.0, 6.0, ((0, 2), (1, 4)))
    cache_mid = noise(part_keys[1], (2, H, W, C1), 1.0, 6.0, ((1, 4),))
    cache_low = noise(part_keys[2], (2, 2 * H, 2 * W, C2), 1.0, 6.0, ((1, 4),))
    gain_mid = jnp.clip(1.0 + 0.18 * jax.random.normal(seeds[3], (C1,), jnp.float32), 0.1, 1.9)
    gain_attn = jnp.clip(1.0 + 0.18 * jax.random.normal(seeds[4], (C1,), jnp.float32), 0.1, 1.9)
    gain_low = jnp.clip(1.0 + 0.18 * jax.random.normal(seeds[5], (C2,), jnp.float32), 0.1, 1.9)
    conv_mid = noise(seeds[6], (3, 3, 3, C1, C1), (27 * C1) ** -0.5, 0.0625, ((4, 2),))
    attn_qkv = draw_attn_qkv(jax.random.fold_in(seeds[11], 71), part)
    attn_proj = noise(seeds[8], (C1, C1), C1 ** -0.5, 0.3125)
    conv_up = noise(seeds[9], (3, 3, C1, C2), (9 * C1) ** -0.5, 0.109375, ((3, 2),))
    conv_low = noise(seeds[10], (3, 3, 3, C2, C2), (27 * C2) ** -0.5, 0.078125, ((4, 2),))
    return dict(latent=latent, cache_mid=cache_mid, cache_low=cache_low, gain_mid=gain_mid, gain_attn=gain_attn, gain_low=gain_low, conv_mid=conv_mid, attn_qkv=attn_qkv, attn_proj=attn_proj, conv_up=conv_up, conv_low=conv_low)


def rms_scaled(values, scales):
    floated = values.astype(jnp.float32)
    return floated * lax.rsqrt(lax.optimization_barrier(jnp.mean(floated * floated, axis=-1, keepdims=True)) + 1e-06) * scales.astype(jnp.float32)

def causal_conv(sequence, kernel):
    return lax.conv_general_dilated(sequence[None].astype(jnp.float32), kernel.astype(jnp.float32), (1, 1, 1), ((0, 0), (1, 1), (1, 1)), dimension_numbers=('NDHWC', 'DHWIO', 'NDHWC'), precision=lax.Precision.HIGHEST)[0]

def reference(latent, cache_mid, cache_low, gain_mid, gain_attn, gain_low, conv_mid, attn_qkv, attn_proj, conv_up, conv_low):
    mid_in = jax.nn.silu(rms_scaled(latent, gain_mid)).astype(jnp.bfloat16)
    mid_seq = jnp.concatenate([cache_mid, mid_in], axis=0)
    segment_one = (latent.astype(jnp.float32) + causal_conv(mid_seq, conv_mid)).astype(jnp.bfloat16)
    attn_in = rms_scaled(segment_one, gain_attn).astype(jnp.bfloat16).reshape(F, H * W, C1)

    def one_frame(frame):
        qkv = jnp.dot(frame, attn_qkv, preferred_element_type=jnp.float32).astype(jnp.bfloat16)
        query = qkv[:, :C1]
        keys = qkv[:, C1:2 * C1]
        vals = qkv[:, 2 * C1:]
        scores = jnp.dot(query, keys.T, preferred_element_type=jnp.float32) / math.sqrt(C1)
        weights = jax.nn.softmax(scores, axis=-1).astype(jnp.bfloat16)
        mixed = jnp.dot(weights, vals, preferred_element_type=jnp.float32).astype(jnp.bfloat16)
        return jnp.dot(mixed, attn_proj, preferred_element_type=jnp.float32)
    branch = lax.map(one_frame, attn_in).reshape(F, H, W, C1)
    segment_two = (segment_one.astype(jnp.float32) + branch).astype(jnp.bfloat16)
    doubled = jnp.repeat(jnp.repeat(segment_two, 2, axis=1), 2, axis=2)
    upper = lax.conv_general_dilated(doubled.astype(jnp.float32), conv_up.astype(jnp.float32), (1, 1), ((1, 1), (1, 1)), dimension_numbers=('NHWC', 'HWIO', 'NHWC'), precision=lax.Precision.HIGHEST).astype(jnp.bfloat16)
    low_in = jax.nn.silu(rms_scaled(upper, gain_low)).astype(jnp.bfloat16)
    low_seq = jnp.concatenate([cache_low, low_in], axis=0)
    return (upper.astype(jnp.float32) + causal_conv(low_seq, conv_low)).astype(jnp.bfloat16)
```

```python
import functools
import math

import jax
import jax.numpy as jnp
from jax import lax
from jax.experimental import pallas as pl
from jax.experimental.pallas import tpu as pltpu
from jax.sharding import PartitionSpec as P

MESH = pl.DeviceIdType.MESH
BF = jnp.bfloat16
F32 = jnp.float32


class Place:
    def __init__(self):
        self.rows, self.segs = lax.axis_size("rows"), lax.axis_size("segment")
        self.z, self.s, self.c = (lax.axis_index(a) for a in ("rows", "segment", "chan"))
        self.up, self.down = self.z > 0, self.z < self.rows - 1
        self.has_next, self.has_prev = self.s < self.segs - 1, self.s > 0

    def greet(self, wide, across):
        barrier = pltpu.get_barrier_semaphore()
        n = jnp.int32(1)
        pl.semaphore_signal(barrier, inc=1, device_id={"chan": 1 - self.c}, device_id_type=MESH)
        for ok, z in ((self.up, self.z - 1), (self.down, self.z + 1)):
            targets = [{"rows": z}]
            if wide:
                targets.append({"rows": z, "chan": 1 - self.c})
            for target in targets:

                @pl.when(ok)
                def _():
                    pl.semaphore_signal(barrier, inc=1, device_id=target, device_id_type=MESH)

            n = n + ok.astype(jnp.int32) * len(targets)
        if across:
            for ok, s in ((self.has_next, self.s + 1), (self.has_prev, self.s - 1)):

                @pl.when(ok)
                def _():
                    pl.semaphore_signal(barrier, inc=1, device_id={"segment": s}, device_id_type=MESH)

                n = n + ok.astype(jnp.int32)
        pl.semaphore_wait(barrier, n)


def remote(src, dst, send, recv, target):
    return pltpu.make_async_remote_copy(
        src_ref=src, dst_ref=dst, send_sem=send, recv_sem=recv, device_id=target, device_id_type=MESH
    )


class Spread:
    def __init__(self, here, src, buf, send, recv):
        c, z, last = here.c, here.z, buf.shape[0] - 1
        self.here = here
        self.partner = remote(src, buf.at[1 + c], send.at[0], recv.at[0], {"chan": 1 - c})
        self.low = [
            remote(src, buf.at[last], send.at[1 + k], recv.at[1], {"rows": z - 1, "chan": k}) for k in (0, 1)
        ]
        self.high = [
            remote(src, buf.at[0], send.at[1 + k], recv.at[2], {"rows": z + 1, "chan": k}) for k in (0, 1)
        ]

    def each(self, act):
        here = self.here

        @pl.when((here.c == 0) & here.up)
        def _():
            for copy in self.low:
                act(copy)

        @pl.when((here.c == 1) & here.down)
        def _():
            for copy in self.high:
                act(copy)

        act(self.partner)

    def start(self):
        self.each(lambda copy: copy.start())

    def wait_send(self):
        self.each(lambda copy: copy.wait_send())

    def wait_recv(self, when=True):
        here = self.here
        self.partner.wait_recv()

        @pl.when(here.down)
        def _():
            self.low[0].wait_recv()

        @pl.when(here.up)
        def _():
            self.high[0].wait_recv()


def normed(v, gain):
    return v * lax.rsqrt(jnp.mean(v * v, axis=-1, keepdims=True) + 1e-06) * gain


def silu(v):
    return v / (1.0 + jnp.exp(-v))


def stored_shifts(x, dst, width):
    n, ch = x.shape
    col = lax.broadcasted_iota(jnp.int32, (n, ch), 0)
    dst[:, :ch] = jnp.where(col == 0, 0.0, pltpu.roll(x, 1, 0)).astype(BF)
    dst[:, ch : 2 * ch] = x.astype(BF)
    dst[:, 2 * ch :] = jnp.where(col == n - 1, 0.0, pltpu.roll(x, n - 1, 0)).astype(BF)


def dot(a, b):
    return jnp.dot(a, b, preferred_element_type=F32)


def picker(rows, cols, hit):
    k = lax.broadcasted_iota(jnp.int32, (rows, cols), 0)
    n = lax.broadcasted_iota(jnp.int32, (rows, cols), 1)
    return jnp.where(hit(k, n), 1.0, 0.0).astype(BF)


def first_kernel(
    latent, cache, gain_mid, gain_attn, w, mine_out, attn_out,
    halo, prior, x3, acc, halfs, hs, hr, xs, xr, ps, pr, es, er, ls,
):
    here = Place()
    frames, rows, width, ch = latent.shape
    part = w.shape[-1]
    c, z = here.c, here.z
    here.greet(True, True)
    to_up = remote(latent.at[:, 0], halo.at[1], hs.at[0], hr.at[0], {"rows": z - 1})
    to_down = remote(latent.at[:, rows - 1], halo.at[0], hs.at[1], hr.at[1], {"rows": z + 1})
    across = remote(latent.at[:, c], prior.at[1 + c], xs, xr, {"segment": here.s + 1})
    local = pltpu.make_async_copy(cache.at[:, c], prior.at[1 + c], ls)
    spread = Spread(here, prior.at[1 + c], prior, ps, pr)

    pl.when(here.has_next)(lambda: across.start())
    pl.when(here.up)(lambda: to_up.start())
    pl.when(here.down)(lambda: to_down.start())

    @pl.when(jnp.logical_not(here.has_prev))
    def _():
        local.start()
        local.wait()

    gain = gain_mid[...]

    def fill(slot, row, x, active):
        v = x.astype(F32)
        if active:
            v = silu(normed(v, gain))
        stored_shifts(v, x3.at[slot, row], width)

    for f in range(frames):
        for r in range(rows):
            fill(frames + f, 1 + r, latent[f, r], True)

    @pl.when(here.has_prev)
    def _():
        across.wait_recv()

    spread.start()
    for ok, copy, k in ((here.up, to_down, 0), (here.down, to_up, 1)):
        row = 0 if k == 0 else rows + 1

        @pl.when(ok)
        def _():
            copy.wait_recv()
            for f in range(frames):
                fill(frames + f, row, halo[k, f], True)

        @pl.when(jnp.logical_not(ok))
        def _():
            for f in range(frames):
                x3[frames + f, row] = jnp.zeros((width, 3 * ch), BF)

    pick = picker(ch, part, lambda k, n: k == n + c * part)
    acc[...] = dot(latent[...].reshape(-1, ch), pick)

    def tap(kt, kh):
        x = x3[pl.ds(kt, frames), pl.ds(kh, rows)].reshape(frames * rows * width, 3 * ch)
        acc[...] += dot(x, w[kt, kh])

    taps_t, taps_h = w.shape[:2]
    lax.fori_loop(0, taps_h, lambda i, _: (tap(taps_t - 1, i), 0)[1], 0)
    spread.wait_recv()
    for row in range(rows + 2):
        inside = True if 0 < row <= rows else (here.up if row == 0 else here.down)
        known = jnp.logical_and(here.z >= 0, inside)
        for active in (False, True):
            origin = here.has_prev if active else jnp.logical_not(here.has_prev)

            @pl.when(known & origin)
            def _():
                for f in range(frames):
                    fill(f, row, prior[row, f], active)

        if row in (0, rows + 1):

            @pl.when(jnp.logical_not(inside))
            def _():
                for f in range(frames):
                    x3[f, row] = jnp.zeros((width, 3 * ch), BF)

    def rest(i, _):
        tap(i // taps_h, i % taps_h)
        return 0

    lax.fori_loop(0, (taps_t - 1) * taps_h, rest, 0)
    result = acc[...].astype(BF).reshape(frames, rows, width, part)
    halfs[0] = jnp.where(c == 0, result[:, 1].astype(F32), result[:, 0].astype(F32)).astype(BF)
    swap = remote(halfs.at[0], halfs.at[1], es, er, {"chan": 1 - c})
    swap.start()
    kept = jnp.where(c == 0, result[:, 0].astype(F32), result[:, 1].astype(F32)).astype(BF)
    put = [picker(part, ch, lambda k, n: n == k + off * part) for off in (c, 1 - c)]
    full = dot(kept.reshape(-1, part), put[0])
    swap.wait()
    full = full + dot(halfs[1].reshape(-1, part), put[1])
    mine_out[...] = full.astype(BF).reshape(frames, width, ch)
    attn_out[...] = normed(full, gain_attn[...]).astype(BF).reshape(frames, width, ch)
    spread.wait_send()
    pl.when(here.has_next)(lambda: across.wait_send())
    pl.when(here.up)(lambda: to_up.wait_send())
    pl.when(here.down)(lambda: to_down.wait_send())


def attn_kernel(mine, attn_in, wqkv, wproj, out, every, scores, values, query, send, recv):
    here = Place()
    frames, width, ch = attn_in.shape
    z, c, chips = here.z, here.c, here.rows
    here.greet(False, False)

    def copy(src, row, f, kind, target):
        return remote(src, every.at[row, f], send.at[row, f, kind], recv.at[row, f], target)

    links = ((0, here.down, {"rows": z + 1}), (1, here.up, {"rows": z - 1}))
    partner = {"chan": 1 - c}
    own = 2 * z + c
    for f in range(frames):
        for kind, ok, target in links:
            pl.when(ok)(lambda: copy(attn_in.at[f], own, f, kind, target).start())
        copy(attn_in.at[f], own, f, 2, partner).start()

    scale = 1.0 / math.sqrt(ch)

    def process(row, f, x):
        kv = dot(x, wqkv[:, ch:]).astype(BF)
        values[row, f] = kv[:, ch:]
        scores[row, f] = (
            lax.dot_general(query[f], kv[:, :ch], (((1,), (1,)), ((), ())), preferred_element_type=F32) * scale
        )

    for f in range(frames):
        query[f] = dot(attn_in[f], wqkv[:, :ch]).astype(BF)
        process(own, f, attn_in[f])

    def other(row, f):
        copy(attn_in.at[f], row, f, 2, partner).wait_recv()
        process(row, f, every[row, f])

    for f in range(frames):
        other(2 * z + 1 - c, f)

    def hop(k, _):
        sides = ((z - k, z - k >= 0, links[0]), (z + k, z + k < chips, links[1]))
        for f in range(frames):
            for src, valid, (kind, ok, target) in sides:
                row = 2 * src + c

                @pl.when(valid)
                def _():
                    copy(attn_in.at[f], row, f, kind, target).wait_recv()
                    copy(every.at[row, f], row, f, 2, partner).start()

                    @pl.when(ok)
                    def _():
                        copy(every.at[row, f], row, f, kind, target).start()

        for src, valid, _ in sides:

            @pl.when(valid)
            def _():
                for f in range(frames):
                    process(2 * src + c, f, every[2 * src + c, f])
                for f in range(frames):
                    other(2 * src + 1 - c, f)

        return 0

    lax.fori_loop(1, chips, hop, 0)

    for f in range(frames):
        part = scores[:, f]
        top = jnp.max(jnp.max(part, axis=0), axis=-1, keepdims=True)
        e = jnp.exp(part - top[None])
        total = jnp.sum(jnp.sum(e, axis=0), axis=-1, keepdims=True)
        weights = (e / total[None]).astype(BF)
        mixed = jnp.zeros((width, ch), F32)
        for row in range(2 * chips):
            mixed = mixed + dot(weights[row], values[row, f])
        out[f] = (mine[f].astype(F32) + dot(mixed.astype(BF), wproj[...])).astype(BF)

    for f in range(frames):
        for kind, ok, target in links:
            pl.when(ok)(lambda: copy(attn_in.at[f], own, f, kind, target).wait_send())
        copy(attn_in.at[f], own, f, 2, partner).wait_send()

    def drain(k, _):
        for f in range(frames):
            for src, valid, (kind, ok, target) in (
                (z - k, z - k >= 0, links[0]),
                (z + k, z + k < chips, links[1]),
            ):
                row = 2 * src + c

                @pl.when(valid)
                def _():
                    copy(every.at[row, f], row, f, 2, partner).wait_send()

                    @pl.when(ok)
                    def _():
                        copy(every.at[row, f], row, f, kind, target).wait_send()

        return 0

    lax.fori_loop(1, chips, drain, 0)


def last_kernel(
    second, cache, gain, wup, wlow, out,
    own, prior, chalo, wother, wmix, wtap, grid, x, upper, acc, ss, sr, xs, xr, ps, pr, cs, cr, ws, wr, ls,
):
    here = Place()
    frames, width, ch = second.shape
    c, z = here.c, here.z
    tall = cache.shape[1]
    two = cache.shape[-1]
    low = two // 2
    part = wup.shape[-1]
    first = jnp.logical_not(here.has_prev)
    here.greet(True, True)
    across = remote(second, prior.at[1 + c], xs, xr, {"segment": here.s + 1})
    local = pltpu.make_async_copy(second, own.at[1 + c], ls)
    spread = Spread(here, second, own, ss, sr)
    relay = Spread(here, prior.at[1 + c], prior, ps, pr)
    to_up = remote(cache.at[:, 0], chalo.at[1], cs.at[0], cr.at[0], {"rows": z - 1})
    to_down = remote(cache.at[:, tall - 1], chalo.at[0], cs.at[1], cr.at[1], {"rows": z + 1})
    weights = remote(wup, wother, ws, wr, {"chan": 1 - c})

    pl.when(here.has_next)(lambda: across.start())
    spread.start()
    weights.start()
    local.start()
    pl.when(first & here.up)(lambda: to_up.start())
    pl.when(first & here.down)(lambda: to_down.start())

    taps_t, taps_h = wlow.shape[:2]

    def lay(i, _):
        kt, kh = i // taps_h, i % taps_h
        tap = [wlow[kt, kh, k * low : (k + 1) * low] for k in range(3)]
        none = jnp.zeros((low, part), BF)
        blocks = ((tap[1], tap[0]), (tap[2], tap[1]), (none, tap[2]), (tap[0], none))
        for at, (even, odd) in enumerate(blocks):
            wtap[kt, kh, at * low : (at + 1) * low, :] = jnp.concatenate([even, odd], axis=1)
        return 0

    lax.fori_loop(0, taps_t * taps_h, lay, 0)

    weights.wait_recv()
    swap = c == 1
    for kh in range(3):
        full = []
        for kw in range(3):
            a, b = wup[kh, kw].astype(F32), wother[kh, kw].astype(F32)
            full.append(jnp.concatenate([jnp.where(swap, b, a), jnp.where(swap, a, b)], axis=1))
        for at, (even, odd) in enumerate(((1, 1), (2, 0), (0, 2))):
            wmix[kh, at] = jnp.concatenate([full[even], full[odd]], axis=1).astype(BF)

    for edge, inside in ((0, here.up), (own.shape[0] - 1, here.down)):

        @pl.when(jnp.logical_not(inside))
        def _():
            own[edge] = jnp.zeros(own.shape[1:], BF)
            prior[edge] = jnp.zeros(own.shape[1:], BF)

    local.wait()
    spread.wait_recv()

    @pl.when(here.has_prev)
    def _():
        across.wait_recv()
        relay.start()

    gains = gain[...]
    lane = lax.broadcasted_iota(jnp.int32, (width, two), 1)
    col = lax.broadcasted_iota(jnp.int32, (width, two), 0)
    evens = lane < low

    def spaced(v, keep_first, keep_last):
        v_next = jnp.where(col == width - 1, 0.0, pltpu.roll(v, width - 1, 0))
        v_prev = jnp.where(col == 0, 0.0, pltpu.roll(v, 1, 0))
        return jnp.where(evens, keep_first(v_prev, v_next), keep_last(v_prev, v_next))

    def put(slot, row, v):
        x[slot, row, :, :two] = v.astype(BF)
        x[slot, row, :, two:] = spaced(v, lambda p, n: n, lambda p, n: p).astype(BF)

    height = own.shape[0]

    def raise_frame(tile, f, slot, keep):
        flat = tile[:, f].reshape(height * width, ch)
        for kh in range(3):
            grid[kh, :, :, :two] = (dot(flat, wmix[kh, 0]) + dot(flat, wmix[kh, 1])).reshape(height, width, two)
            grid[kh, :, :, two:] = dot(flat, wmix[kh, 2]).reshape(height, width, two)
        for r in range(tall + 2):
            i, odd = (r + 1) // 2, (r + 1) % 2
            sources = (i, i, i + 1) if odd else (i - 1, i, i)
            both = sum(grid[kh, sources[kh]] for kh in range(3))
            v = both[:, :two] + spaced(both[:, two:], lambda p, n: p, lambda p, n: n)
            v = v.astype(BF)
            if keep and 0 < r <= tall:
                upper[f, r - 1] = v
            v = v.astype(F32)
            sq = v * v
            mean_even = jnp.sum(jnp.where(evens, sq, 0.0), axis=-1, keepdims=True) / low
            mean_odd = jnp.sum(jnp.where(evens, 0.0, sq), axis=-1, keepdims=True) / low
            v = v * jnp.where(evens, lax.rsqrt(mean_even + 1e-06), lax.rsqrt(mean_odd + 1e-06)) * gains
            v = silu(v)
            if r == 0:
                v = jnp.where(here.up, v, 0.0)
            if r == tall + 1:
                v = jnp.where(here.down, v, 0.0)
            put(slot, r, v.astype(BF).astype(F32))

    lax.fori_loop(0, frames, lambda f, _: (raise_frame(own, f, frames + f, True), 0)[1], 0)

    n = 2 * part
    pick = picker(two, n, lambda k, j: k == jnp.where(j < part, j, j - part + low) + c * part)
    acc[...] = dot(upper[...].reshape(-1, two), pick)

    def tap(kt, kh):
        v = x[pl.ds(kt, frames), pl.ds(kh, tall)].reshape(frames * tall * width, 2 * two)
        acc[...] += dot(v, wtap[kt, kh])

    lax.fori_loop(0, taps_h, lambda i, _: (tap(taps_t - 1, i), 0)[1], 0)

    @pl.when(here.has_prev)
    def _():
        relay.wait_recv()
        lax.fori_loop(0, frames, lambda f, _: (raise_frame(prior, f, f, False), 0)[1], 0)

    @pl.when(first)
    def _():
        def take(i, _):
            put(i // tall, 1 + i % tall, cache[i // tall, i % tall].astype(F32))
            return 0

        lax.fori_loop(0, frames * tall, take, 0)

    for row, inside, k, copy in ((0, here.up, 0, to_down), (tall + 1, here.down, 1, to_up)):

        @pl.when(first & inside)
        def _():
            copy.wait_recv()
            for f in range(frames):
                put(f, row, chalo[k, f].astype(F32))

        @pl.when(first & jnp.logical_not(inside))
        def _():
            for f in range(frames):
                put(f, row, jnp.zeros((width, two), F32))

    def rest(i, _):
        tap(i // taps_h, i % taps_h)
        return 0

    lax.fori_loop(0, (taps_t - 1) * taps_h, rest, 0)
    out[...] = acc[...].astype(BF).reshape(out.shape)
    spread.wait_send()
    weights.wait_send()
    pl.when(here.has_prev)(lambda: relay.wait_send())
    pl.when(here.has_next)(lambda: across.wait_send())
    pl.when(first & here.up)(lambda: to_up.wait_send())
    pl.when(first & here.down)(lambda: to_down.wait_send())


def call(kernel, number, outs, scratch, *args):
    return pl.pallas_call(
        kernel,
        out_shape=outs,
        in_specs=[pl.BlockSpec(memory_space=pltpu.VMEM)] * len(args),
        out_specs=jax.tree.map(lambda _: pl.BlockSpec(memory_space=pltpu.VMEM), outs),
        scratch_shapes=scratch,
        compiler_params=pltpu.CompilerParams(
            collective_id=number, has_side_effects=True, vmem_limit_bytes=60 * 1024 * 1024
        ),
    )(*args)


def body(
    latent, cache_mid, cache_low, gain_mid, gain_attn, gain_low, conv_mid, attn_qkv, attn_proj, conv_up, conv_low
):
    frames, rows, width, ch = latent.shape
    part = conv_mid.shape[-1]
    dma, one = pltpu.SemaphoreType.DMA, pltpu.SemaphoreType.DMA(())
    row = jax.ShapeDtypeStruct((frames, width, ch), BF)
    taps_t, taps_h, taps_w = conv_mid.shape[:3]
    mine, attn_in = call(
        first_kernel,
        0,
        (row, row),
        [
            pltpu.VMEM((2, frames, width, ch), BF),
            pltpu.VMEM((rows + 2, frames, width, ch), BF),
            pltpu.VMEM((2 * frames, rows + 2, width, taps_w * ch), BF),
            pltpu.VMEM((frames * rows * width, part), F32),
            pltpu.VMEM((2, frames, width, part), BF),
            dma((2,)), dma((2,)), one, one, dma((3,)), dma((3,)), one, one, one,
        ],
        latent,
        cache_mid,
        gain_mid.reshape(1, -1),
        gain_attn.reshape(1, -1),
        conv_mid.reshape(taps_t, taps_h, taps_w * ch, part),
    )
    total = rows * lax.axis_size("rows")
    second = call(
        attn_kernel,
        1,
        row,
        [
            pltpu.VMEM((total, frames, width, ch), BF),
            pltpu.VMEM((total, frames, width, width), F32),
            pltpu.VMEM((total, frames, width, ch), BF),
            pltpu.VMEM((frames, width, ch), BF),
            dma((total, frames, 3)),
            dma((total, frames)),
        ],
        mine,
        attn_in,
        attn_qkv,
        attn_proj,
    )
    _, tall, wide, low = cache_low.shape
    cut = conv_low.shape[-1]
    two = 2 * low
    taps_t, taps_h, taps_w = conv_low.shape[:3]
    decoded = call(
        last_kernel,
        2,
        jax.ShapeDtypeStruct((frames, tall, width, 2 * cut), BF),
        [
            pltpu.VMEM((rows + 2, frames, width, ch), BF),
            pltpu.VMEM((rows + 2, frames, width, ch), BF),
            pltpu.VMEM((2, frames, width, two), BF),
            pltpu.VMEM(conv_up.shape, BF),
            pltpu.VMEM((3, 3, ch, two), BF),
            pltpu.VMEM((taps_t, taps_h, 2 * two, 2 * cut), BF),
            pltpu.VMEM((3, rows + 2, width, 2 * two), F32),
            pltpu.VMEM((2 * frames, tall + 2, width, 2 * two), BF),
            pltpu.VMEM((frames, tall, width, two), BF),
            pltpu.VMEM((frames * tall * width, 2 * cut), F32),
            dma((3,)), dma((3,)), one, one, dma((3,)), dma((3,)), dma((2,)), dma((2,)), one, one, one,
        ],
        second,
        cache_low.reshape(frames, tall, width, two),
        jnp.concatenate([gain_low, gain_low]).reshape(1, -1),
        conv_up,
        conv_low.reshape(taps_t, taps_h, taps_w * low, cut),
    )
    return decoded.reshape(frames, tall, wide, cut)


def solution(mesh):
    placed = (
        P(("groups", "segment"), "rows", None, None),
        P("groups", "rows", None, None),
        P("groups", "rows", None, None),
        P(),
        P(),
        P(),
        P(None, None, None, None, "chan"),
        P(),
        P(),
        P(None, None, None, "chan"),
        P(None, None, None, None, "chan"),
    )
    return jax.shard_map(
        body,
        mesh=mesh,
        in_specs=placed,
        out_specs=P(("groups", "segment"), "rows", None, "chan"),
        check_vma=False,
    )
```

```python
import functools
import math

import jax
import jax.numpy as jnp
from jax import lax
from jax.experimental import pallas as pl
from jax.experimental.pallas import tpu as pltpu
from jax.sharding import PartitionSpec as P

MESH = pl.DeviceIdType.MESH
BF = jnp.bfloat16
F32 = jnp.float32


class Place:
    def __init__(self):
        self.rows, self.segs = lax.axis_size("rows"), lax.axis_size("segment")
        self.z, self.s, self.c = (lax.axis_index(a) for a in ("rows", "segment", "chan"))
        self.up, self.down = self.z > 0, self.z < self.rows - 1
        self.has_next, self.has_prev = self.s < self.segs - 1, self.s > 0

    def greet(self, wide, across):
        barrier = pltpu.get_barrier_semaphore()
        n = jnp.int32(1)
        pl.semaphore_signal(barrier, inc=1, device_id={"chan": 1 - self.c}, device_id_type=MESH)
        for ok, z in ((self.up, self.z - 1), (self.down, self.z + 1)):
            targets = [{"rows": z}]
            if wide:
                targets.append({"rows": z, "chan": 1 - self.c})
            for target in targets:

                @pl.when(ok)
                def _():
                    pl.semaphore_signal(barrier, inc=1, device_id=target, device_id_type=MESH)

            n = n + ok.astype(jnp.int32) * len(targets)
        if across:
            for ok, s in ((self.has_next, self.s + 1), (self.has_prev, self.s - 1)):

                @pl.when(ok)
                def _():
                    pl.semaphore_signal(barrier, inc=1, device_id={"segment": s}, device_id_type=MESH)

                n = n + ok.astype(jnp.int32)
        pl.semaphore_wait(barrier, n)


def remote(src, dst, send, recv, target):
    return pltpu.make_async_remote_copy(
        src_ref=src, dst_ref=dst, send_sem=send, recv_sem=recv, device_id=target, device_id_type=MESH
    )


class Spread:
    def __init__(self, here, src, buf, send, recv):
        c, z, last = here.c, here.z, buf.shape[0] - 1
        self.here = here
        self.partner = remote(src, buf.at[1 + c], send.at[0], recv.at[0], {"chan": 1 - c})
        self.low = [
            remote(src, buf.at[last], send.at[1 + k], recv.at[1], {"rows": z - 1, "chan": k}) for k in (0, 1)
        ]
        self.high = [
            remote(src, buf.at[0], send.at[1 + k], recv.at[2], {"rows": z + 1, "chan": k}) for k in (0, 1)
        ]

    def each(self, act):
        here = self.here

        @pl.when((here.c == 0) & here.up)
        def _():
            for copy in self.low:
                act(copy)

        @pl.when((here.c == 1) & here.down)
        def _():
            for copy in self.high:
                act(copy)

        act(self.partner)

    def start(self):
        self.each(lambda copy: copy.start())

    def wait_send(self):
        self.each(lambda copy: copy.wait_send())

    def wait_recv(self, when=True):
        here = self.here
        self.partner.wait_recv()

        @pl.when(here.down)
        def _():
            self.low[0].wait_recv()

        @pl.when(here.up)
        def _():
            self.high[0].wait_recv()


def normed(v, gain):
    return v * lax.rsqrt(jnp.mean(v * v, axis=-1, keepdims=True) + 1e-06) * gain


def silu(v):
    return 0.5 * v * (1.0 + jnp.tanh(0.5 * v))


def stored_shifts(x, dst, width):
    n, ch = x.shape
    col = lax.broadcasted_iota(jnp.int32, (n, ch), 0)
    dst[:, :ch] = jnp.where(col == 0, 0.0, pltpu.roll(x, 1, 0)).astype(BF)
    dst[:, ch : 2 * ch] = x.astype(BF)
    dst[:, 2 * ch :] = jnp.where(col == n - 1, 0.0, pltpu.roll(x, n - 1, 0)).astype(BF)


def dot(a, b):
    return jnp.dot(a, b, preferred_element_type=F32)


def dot_t(a, b):
    return lax.dot_general(a, b, (((1,), (1,)), ((), ())), preferred_element_type=F32)


def picker(rows, cols, hit):
    k = lax.broadcasted_iota(jnp.int32, (rows, cols), 0)
    n = lax.broadcasted_iota(jnp.int32, (rows, cols), 1)
    return jnp.where(hit(k, n), 1.0, 0.0).astype(BF)


def first_kernel(
    latent, cache, gain_mid, gain_attn, w_hbm, mine_out, attn_out,
    w, halo, prior, x3, acc, halfs, hs, hr, xs, xr, ps, pr, es, er, ls, wsem,
):
    here = Place()
    frames, rows, width, ch = latent.shape
    part = w.shape[-2]
    c, z = here.c, here.z
    fetch = pltpu.make_async_copy(w_hbm, w, wsem)
    fetch.start()
    here.greet(True, True)
    to_up = remote(latent.at[:, 0], halo.at[1], hs.at[0], hr.at[0], {"rows": z - 1})
    to_down = remote(latent.at[:, rows - 1], halo.at[0], hs.at[1], hr.at[1], {"rows": z + 1})
    across = remote(latent.at[:, c], prior.at[1 + c], xs, xr, {"segment": here.s + 1})
    local = pltpu.make_async_copy(cache.at[:, c], prior.at[1 + c], ls)
    spread = Spread(here, prior.at[1 + c], prior, ps, pr)

    pl.when(here.has_next)(lambda: across.start())
    pl.when(here.up)(lambda: to_up.start())
    pl.when(here.down)(lambda: to_down.start())

    @pl.when(jnp.logical_not(here.has_prev))
    def _():
        local.start()
        local.wait()

    gain = gain_mid[...].reshape(1, ch)

    def fill(slot, row, x, active):
        v = x.astype(F32)
        if active:
            v = silu(normed(v, gain))
        stored_shifts(v, x3.at[slot, row], width)

    for f in range(frames):
        for r in range(rows):
            fill(frames + f, 1 + r, latent[f, r], True)

    @pl.when(here.has_prev)
    def _():
        across.wait_recv()

    spread.start()
    for ok, copy, k in ((here.up, to_down, 0), (here.down, to_up, 1)):
        row = 0 if k == 0 else rows + 1

        @pl.when(ok)
        def _():
            copy.wait_recv()
            for f in range(frames):
                fill(frames + f, row, halo[k, f], True)

        @pl.when(jnp.logical_not(ok))
        def _():
            for f in range(frames):
                x3[frames + f, row] = jnp.zeros((width, 3 * ch), BF)

    pick = picker(ch, part, lambda k, n: k == n + c * part)
    acc[...] = dot(latent[...].reshape(-1, ch), pick)

    def tap(kt, kh):
        x = x3[pl.ds(kt, frames), pl.ds(kh, rows)].reshape(frames * rows * width, 3 * ch)
        acc[...] += sum(dot_t(x[:, k * ch : (k + 1) * ch], w[kt, kh, k]) for k in range(3))

    taps_t, taps_h = w.shape[:2]
    fetch.wait()
    lax.fori_loop(0, taps_h, lambda i, _: (tap(taps_t - 1, i), 0)[1], 0)
    spread.wait_recv()
    for row in range(rows + 2):
        inside = True if 0 < row <= rows else (here.up if row == 0 else here.down)
        known = jnp.logical_and(here.z >= 0, inside)
        for active in (False, True):
            origin = here.has_prev if active else jnp.logical_not(here.has_prev)

            @pl.when(known & origin)
            def _():
                for f in range(frames):
                    fill(f, row, prior[row, f], active)

        if row in (0, rows + 1):

            @pl.when(jnp.logical_not(inside))
            def _():
                for f in range(frames):
                    x3[f, row] = jnp.zeros((width, 3 * ch), BF)

    def rest(i, _):
        tap(i // taps_h, i % taps_h)
        return 0

    lax.fori_loop(0, (taps_t - 1) * taps_h, rest, 0)
    result = acc[...].astype(BF).reshape(frames, rows, width, part)
    halfs[0] = jnp.where(c == 0, result[:, 1].astype(F32), result[:, 0].astype(F32)).astype(BF)
    swap = remote(halfs.at[0], halfs.at[1], es, er, {"chan": 1 - c})
    swap.start()
    kept = jnp.where(c == 0, result[:, 0].astype(F32), result[:, 1].astype(F32)).astype(BF)
    put = [picker(part, ch, lambda k, n: n == k + off * part) for off in (c, 1 - c)]
    full = dot(kept.reshape(-1, part), put[0])
    swap.wait()
    full = full + dot(halfs[1].reshape(-1, part), put[1])
    mine_out[...] = full.astype(BF).reshape(frames, width, ch)
    attn_out[...] = normed(full, gain_attn[...].reshape(1, ch)).astype(BF).reshape(frames, width, ch)
    spread.wait_send()
    pl.when(here.has_next)(lambda: across.wait_send())
    pl.when(here.up)(lambda: to_up.wait_send())
    pl.when(here.down)(lambda: to_down.wait_send())


def attn_kernel(mine, attn_in, wqkv, wproj, out, every, scores, values, query, send, recv):
    here = Place()
    frames, width, ch = attn_in.shape
    z, c, chips = here.z, here.c, here.rows
    here.greet(False, False)

    def copy(src, row, f, kind, target):
        return remote(src, every.at[row, f], send.at[row, f, kind], recv.at[row, f], target)

    links = ((0, here.down, {"rows": z + 1}), (1, here.up, {"rows": z - 1}))
    partner = {"chan": 1 - c}
    own = 2 * z + c
    for f in range(frames):
        for kind, ok, target in links:
            pl.when(ok)(lambda: copy(attn_in.at[f], own, f, kind, target).start())
        copy(attn_in.at[f], own, f, 2, partner).start()

    scale = 1.0 / math.sqrt(ch)

    def process(row, f, x):
        kv = dot(x, wqkv[:, ch:]).astype(BF)
        values[row, f] = kv[:, ch:]
        scores[row, f] = (
            lax.dot_general(query[f], kv[:, :ch], (((1,), (1,)), ((), ())), preferred_element_type=F32) * scale
        )

    for f in range(frames):
        query[f] = dot(attn_in[f], wqkv[:, :ch]).astype(BF)
        process(own, f, attn_in[f])

    def other(row, f):
        copy(attn_in.at[f], row, f, 2, partner).wait_recv()
        process(row, f, every[row, f])

    for f in range(frames):
        other(2 * z + 1 - c, f)

    def hop(k, _):
        sides = ((z - k, z - k >= 0, links[0]), (z + k, z + k < chips, links[1]))
        for f in range(frames):
            for src, valid, (kind, ok, target) in sides:
                row = 2 * src + c

                @pl.when(valid)
                def _():
                    copy(attn_in.at[f], row, f, kind, target).wait_recv()
                    copy(every.at[row, f], row, f, 2, partner).start()

                    @pl.when(ok)
                    def _():
                        copy(every.at[row, f], row, f, kind, target).start()

        for src, valid, _ in sides:

            @pl.when(valid)
            def _():
                for f in range(frames):
                    process(2 * src + c, f, every[2 * src + c, f])
                for f in range(frames):
                    other(2 * src + 1 - c, f)

        return 0

    lax.fori_loop(1, chips, hop, 0)

    for f in range(frames):
        part = scores[:, f]
        top = jnp.max(jnp.max(part, axis=0), axis=-1, keepdims=True)
        e = jnp.exp(part - top[None])
        total = jnp.sum(jnp.sum(e, axis=0), axis=-1, keepdims=True)
        weights = (e / total[None]).astype(BF)
        mixed = jnp.zeros((width, ch), F32)
        for row in range(2 * chips):
            mixed = mixed + dot(weights[row], values[row, f])
        out[f] = (mine[f].astype(F32) + dot(mixed.astype(BF), wproj[...])).astype(BF)

    for f in range(frames):
        for kind, ok, target in links:
            pl.when(ok)(lambda: copy(attn_in.at[f], own, f, kind, target).wait_send())
        copy(attn_in.at[f], own, f, 2, partner).wait_send()

    def drain(k, _):
        for f in range(frames):
            for src, valid, (kind, ok, target) in (
                (z - k, z - k >= 0, links[0]),
                (z + k, z + k < chips, links[1]),
            ):
                row = 2 * src + c

                @pl.when(valid)
                def _():
                    copy(every.at[row, f], row, f, 2, partner).wait_send()

                    @pl.when(ok)
                    def _():
                        copy(every.at[row, f], row, f, kind, target).wait_send()

        return 0

    lax.fori_loop(1, chips, drain, 0)


class Deal:
    def __init__(self, here, src, buf, send, recv):
        c, z, last = here.c, here.z, buf.shape[0] - 1
        self.here = here
        self.local = pltpu.make_async_copy(src.at[c], buf.at[1 + c], send.at[3])
        self.partner = remote(src.at[1 - c], buf.at[1 + c], send.at[0], recv.at[0], {"chan": 1 - c})
        self.low = [
            remote(src.at[k], buf.at[last], send.at[1 + k], recv.at[1], {"rows": z - 1, "chan": k}) for k in (0, 1)
        ]
        self.high = [
            remote(src.at[k], buf.at[0], send.at[1 + k], recv.at[2], {"rows": z + 1, "chan": k}) for k in (0, 1)
        ]

    def each(self, act):
        here = self.here

        @pl.when((here.c == 0) & here.up)
        def _():
            for copy in self.low:
                act(copy)

        @pl.when((here.c == 1) & here.down)
        def _():
            for copy in self.high:
                act(copy)

        act(self.partner)

    def start(self):
        self.each(lambda copy: copy.start())
        self.local.start()

    def wait_send(self):
        self.each(lambda copy: copy.wait_send())

    def wait_recv(self):
        here = self.here
        self.local.wait()
        self.partner.wait_recv()
        pl.when(here.down)(lambda: self.low[0].wait_recv())
        pl.when(here.up)(lambda: self.high[0].wait_recv())


def last_kernel(
    second, cache, gain, wup, wlow_hbm, out,
    wlow, own, stage, prior, chalo, wfull, wmix, wtap, grid, x, upper, acc,
    ss, sr, xs, xr, ps, pr, cs, cr, ws, wr, ls, fs, es, er, us, ur,
):
    here = Place()
    frames, width, ch = second.shape
    c, z = here.c, here.z
    tall = cache.shape[1]
    low = cache.shape[2]
    wide = cache.shape[3]
    two = 2 * low
    part = wup.shape[2]
    first = jnp.logical_not(here.has_prev)
    fetch = pltpu.make_async_copy(wlow_hbm, wlow, fs)
    fetch.start()
    local = pltpu.make_async_copy(wup, wfull.at[c], ls)
    local.start()
    here.greet(True, True)
    across = remote(second, stage, xs, xr, {"segment": here.s + 1})
    spread = Deal(here, second, own, ss, sr)
    relay = Deal(here, stage, prior, ps, pr)
    to_up = remote(cache.at[:, 0], chalo.at[1], cs.at[0], cr.at[0], {"rows": z - 1})
    to_down = remote(cache.at[:, tall - 1], chalo.at[0], cs.at[1], cr.at[1], {"rows": z + 1})
    weights = remote(wup, wfull.at[c], ws, wr, {"chan": 1 - c})

    pl.when(here.has_next)(lambda: across.start())
    spread.start()
    weights.start()
    pl.when(first & here.up)(lambda: to_up.start())
    pl.when(first & here.down)(lambda: to_down.start())

    for edge, inside in ((0, here.up), (own.shape[0] - 1, here.down)):

        @pl.when(jnp.logical_not(inside))
        def _():
            own[edge] = jnp.zeros(own.shape[1:], BF)
            prior[edge] = jnp.zeros(own.shape[1:], BF)

    taps_t, taps_h = wlow.shape[:2]
    fetch.wait()

    def lay(i, _):
        kt, kh = i // taps_h, i % taps_h
        tap = [wlow[kt, kh, k * low : (k + 1) * low] for k in range(3)]
        none = jnp.zeros((low, part), BF)
        blocks = ((tap[1], tap[0]), (tap[2], tap[1]), (none, tap[2]), (tap[0], none))
        for at, (even, odd) in enumerate(blocks):
            wtap[kt, kh, at * low : (at + 1) * low, :] = jnp.concatenate([even, odd], axis=1)
        return 0

    lax.fori_loop(0, taps_t * taps_h, lay, 0)

    local.wait()
    weights.wait_recv()
    for kh in range(3):
        for at, sides in enumerate(((1, 1), (2, 0), (0, 2))):
            for side, kw in enumerate(sides):
                for half in (0, 1):
                    start = side * low + half * part
                    wmix[kh, at, start : start + part] = wfull[half, kh, kw]

    spread.wait_recv()

    @pl.when(here.has_prev)
    def _():
        across.wait_recv()
        relay.start()

    gains = gain[...].reshape(1, low)
    gains = jnp.concatenate([gains, gains], axis=1)
    lane = lax.broadcasted_iota(jnp.int32, (width, two), 1)
    col = lax.broadcasted_iota(jnp.int32, (width, two), 0)
    evens = lane < low

    def spaced(v, keep_first, keep_last):
        v_next = jnp.where(col == width - 1, 0.0, pltpu.roll(v, width - 1, 0))
        v_prev = jnp.where(col == 0, 0.0, pltpu.roll(v, 1, 0))
        return jnp.where(evens, keep_first(v_prev, v_next), keep_last(v_prev, v_next))

    def beside(slot, row, v):
        x[slot, row, :, two:] = spaced(v, lambda p, n: n, lambda p, n: p).astype(BF)

    def put(slot, row, v):
        x[slot, row, :, :two] = v.astype(BF)
        beside(slot, row, v)

    height = own.shape[0]

    def row_copy(slot, at, r):
        piece = x.at[slot, r, :, pl.ds(0, two)]
        return remote(piece, piece, es.at[at, r], er.at[at, r], {"chan": 1 - c})

    def upper_copy(f, r):
        return remote(upper.at[f, r], upper.at[f, r], us.at[r], ur.at[r], {"chan": 1 - c})

    def raise_frame(tile, at):
        slot = at * frames + c
        for kh in range(3):
            n0, n1 = (0, height - 1) if kh == 0 else (0, height) if kh == 1 else (1, height)
            flat = tile[n0:n1].reshape((n1 - n0) * width, ch)
            grid[kh, n0:n1, :, :two] = (dot_t(flat, wmix[kh, 0]) + dot_t(flat, wmix[kh, 1])).reshape(
                n1 - n0, width, two
            )
            grid[kh, n0:n1, :, two:] = dot_t(flat, wmix[kh, 2]).reshape(n1 - n0, width, two)
        for r in range(tall + 2):
            i, odd = (r + 1) // 2, (r + 1) % 2
            sources = (i, i, i + 1) if odd else (i - 1, i, i)
            both = sum(grid[kh, sources[kh]] for kh in range(3))
            v = both[:, :two] + spaced(both[:, two:], lambda p, n: p, lambda p, n: n)
            v = v.astype(BF)
            if at and 0 < r <= tall:
                upper[c, r - 1] = v
                upper_copy(c, r - 1).start()
            v = v.astype(F32)
            sq = v * v
            mean_even = jnp.sum(jnp.where(evens, sq, 0.0), axis=-1, keepdims=True) / low
            mean_odd = jnp.sum(jnp.where(evens, 0.0, sq), axis=-1, keepdims=True) / low
            v = v * jnp.where(evens, lax.rsqrt(mean_even + 1e-06), lax.rsqrt(mean_odd + 1e-06)) * gains
            v = silu(v)
            if r == 0:
                v = jnp.where(here.up, v, 0.0)
            if r == tall + 1:
                v = jnp.where(here.down, v, 0.0)
            put(slot, r, v)
            row_copy(slot, at, r).start()
        other = at * frames + 1 - c
        for r in range(tall + 2):
            row_copy(other, at, r).wait_recv()
            beside(other, r, x[other, r, :, :two].astype(F32))

    raise_frame(own, 1)
    acc[...] = jnp.zeros(acc.shape, F32)

    def tap(kt, kh):
        v = x[pl.ds(kt, frames), pl.ds(kh, tall)].reshape(frames * tall * width, 2 * two)
        acc[...] += dot(v, wtap[kt, kh])

    lax.fori_loop(0, taps_h, lambda i, _: (tap(taps_t - 1, i), 0)[1], 0)

    @pl.when(here.has_prev)
    def _():
        relay.wait_recv()
        raise_frame(prior, 0)

    spots = [picker(width, wide, lambda k, n: n == 2 * k + p) for p in (0, 1)]

    def take(slot, row, flipped):
        put(slot, row, jnp.concatenate([dot_t(spot, flipped) for spot in spots], axis=1))

    @pl.when(first)
    def _():
        def each(i, _):
            take(i // tall, 1 + i % tall, cache[i // tall, i % tall])
            return 0

        lax.fori_loop(0, frames * tall, each, 0)

    for row, inside, k, copy in ((0, here.up, 0, to_down), (tall + 1, here.down, 1, to_up)):

        @pl.when(first & inside)
        def _():
            copy.wait_recv()
            for f in range(frames):
                take(f, row, chalo[k, f])

        @pl.when(first & jnp.logical_not(inside))
        def _():
            for f in range(frames):
                put(f, row, jnp.zeros((width, two), F32))

    def rest(i, _):
        tap(i // taps_h, i % taps_h)
        return 0

    lax.fori_loop(0, (taps_t - 1) * taps_h, rest, 0)
    n = 2 * part
    pick = picker(two, n, lambda k, j: k == jnp.where(j < part, j, j - part + low) + c * part)
    for r in range(tall):
        upper_copy(1 - c, r).wait_recv()
    acc[...] += dot(upper[...].reshape(-1, two), pick)

    def finish(i, _):
        done = acc[pl.ds(pl.multiple_of(i * width, width), width), :].T.astype(BF)
        out[i // tall, i % tall] = (dot(done[:part], spots[0]) + dot(done[part:], spots[1])).astype(BF)
        return 0

    lax.fori_loop(0, frames * tall, finish, 0)
    spread.wait_send()
    weights.wait_send()
    for r in range(tall):
        upper_copy(c, r).wait_send()
    for r in range(tall + 2):
        row_copy(frames + c, 1, r).wait_send()

    @pl.when(here.has_prev)
    def _():
        relay.wait_send()
        for r in range(tall + 2):
            row_copy(c, 0, r).wait_send()

    pl.when(here.has_next)(lambda: across.wait_send())
    pl.when(first & here.up)(lambda: to_up.wait_send())
    pl.when(first & here.down)(lambda: to_down.wait_send())


def call(kernel, number, outs, scratch, *args, far=()):
    return pl.pallas_call(
        kernel,
        out_shape=outs,
        in_specs=[pl.BlockSpec(memory_space=pl.ANY if i in far else pltpu.VMEM) for i in range(len(args))],
        out_specs=jax.tree.map(lambda _: pl.BlockSpec(memory_space=pltpu.VMEM), outs),
        scratch_shapes=scratch,
        compiler_params=pltpu.CompilerParams(
            collective_id=number, has_side_effects=True, vmem_limit_bytes=60 * 1024 * 1024
        ),
    )(*args)


def body(
    latent, cache_mid, cache_low, gain_mid, gain_attn, gain_low, conv_mid, attn_qkv, attn_proj, conv_up, conv_low
):
    frames, rows, width, ch = latent.shape
    part = conv_mid.shape[-1]
    dma, one = pltpu.SemaphoreType.DMA, pltpu.SemaphoreType.DMA(())
    row = jax.ShapeDtypeStruct((frames, width, ch), BF)
    taps_t, taps_h, taps_w = conv_mid.shape[:3]
    mine, attn_in = call(
        first_kernel,
        0,
        (row, row),
        [
            pltpu.VMEM((taps_t, taps_h, taps_w, part, ch), BF),
            pltpu.VMEM((2, frames, width, ch), BF),
            pltpu.VMEM((rows + 2, frames, width, ch), BF),
            pltpu.VMEM((2 * frames, rows + 2, width, taps_w * ch), BF),
            pltpu.VMEM((frames * rows * width, part), F32),
            pltpu.VMEM((2, frames, width, part), BF),
            dma((2,)), dma((2,)), one, one, dma((3,)), dma((3,)), one, one, one, one,
        ],
        latent,
        cache_mid,
        gain_mid,
        gain_attn,
        jnp.swapaxes(conv_mid, 3, 4),
        far=(4,),
    )
    total = rows * lax.axis_size("rows")
    second = call(
        attn_kernel,
        1,
        row,
        [
            pltpu.VMEM((total, frames, width, ch), BF),
            pltpu.VMEM((total, frames, width, width), F32),
            pltpu.VMEM((total, frames, width, ch), BF),
            pltpu.VMEM((frames, width, ch), BF),
            dma((total, frames, 3)),
            dma((total, frames)),
        ],
        mine,
        attn_in,
        attn_qkv,
        attn_proj,
    )
    _, tall, wide, low = cache_low.shape
    cut = conv_low.shape[-1]
    two = 2 * low
    taps_t, taps_h, taps_w = conv_low.shape[:3]
    decoded = call(
        last_kernel,
        2,
        jax.ShapeDtypeStruct((frames, tall, cut, wide), BF),
        [
            pltpu.VMEM((taps_t, taps_h, taps_w * low, cut), BF),
            pltpu.VMEM((rows + 2, width, ch), BF),
            pltpu.VMEM((frames, width, ch), BF),
            pltpu.VMEM((rows + 2, width, ch), BF),
            pltpu.VMEM((2, frames, low, wide), BF),
            pltpu.VMEM((2, 3, 3, cut, ch), BF),
            pltpu.VMEM((3, 3, two, ch), BF),
            pltpu.VMEM((taps_t, taps_h, 2 * two, 2 * cut), BF),
            pltpu.VMEM((3, rows + 2, width, 2 * two), F32),
            pltpu.VMEM((2 * frames, tall + 2, width, 2 * two), BF),
            pltpu.VMEM((frames, tall, width, two), BF),
            pltpu.VMEM((frames * tall * width, 2 * cut), F32),
            dma((4,)), dma((3,)), one, one, dma((4,)), dma((3,)), dma((2,)), dma((2,)), one, one, one, one,
            dma((2, tall + 2)), dma((2, tall + 2)), dma((tall,)), dma((tall,)),
        ],
        second,
        jnp.swapaxes(cache_low, 2, 3),
        gain_low,
        jnp.swapaxes(conv_up, 2, 3),
        conv_low.reshape(taps_t, taps_h, taps_w * low, cut),
        far=(4,),
    )
    return jnp.swapaxes(decoded, 2, 3)


def solution(mesh):
    placed = (
        P(("groups", "segment"), "rows", None, None),
        P("groups", "rows", None, None),
        P("groups", "rows", None, None),
        P(),
        P(),
        P(),
        P(None, None, None, None, "chan"),
        P(),
        P(),
        P(None, None, None, "chan"),
        P(None, None, None, None, "chan"),
    )
    return jax.shard_map(
        body,
        mesh=mesh,
        in_specs=placed,
        out_specs=P(("groups", "segment"), "rows", None, "chan"),
        check_vma=False,
    )
```

```python
import functools
import math

import jax
import jax.numpy as jnp
from jax import lax
from jax.experimental import pallas as pl
from jax.experimental.pallas import tpu as pltpu
from jax.sharding import PartitionSpec as P

MESH = pl.DeviceIdType.MESH
BF = jnp.bfloat16
F32 = jnp.float32


class Place:
    def __init__(self):
        self.rows, self.segs = lax.axis_size("rows"), lax.axis_size("segment")
        self.z, self.s, self.c = (lax.axis_index(a) for a in ("rows", "segment", "chan"))
        self.up, self.down = self.z > 0, self.z < self.rows - 1
        self.has_next, self.has_prev = self.s < self.segs - 1, self.s > 0

    def greet(self, wide, across):
        barrier = pltpu.get_barrier_semaphore()
        n = jnp.int32(1)
        pl.semaphore_signal(barrier, inc=1, device_id={"chan": 1 - self.c}, device_id_type=MESH)
        for ok, z in ((self.up, self.z - 1), (self.down, self.z + 1)):
            targets = [{"rows": z}]
            if wide:
                targets.append({"rows": z, "chan": 1 - self.c})
            for target in targets:

                @pl.when(ok)
                def _():
                    pl.semaphore_signal(barrier, inc=1, device_id=target, device_id_type=MESH)

            n = n + ok.astype(jnp.int32) * len(targets)
        if across:
            for ok, s in ((self.has_next, self.s + 1), (self.has_prev, self.s - 1)):

                @pl.when(ok)
                def _():
                    pl.semaphore_signal(barrier, inc=1, device_id={"segment": s}, device_id_type=MESH)

                n = n + ok.astype(jnp.int32)
        pl.semaphore_wait(barrier, n)


def remote(src, dst, send, recv, target):
    return pltpu.make_async_remote_copy(
        src_ref=src, dst_ref=dst, send_sem=send, recv_sem=recv, device_id=target, device_id_type=MESH
    )


class Spread:
    def __init__(self, here, src, buf, send, recv):
        c, z, last = here.c, here.z, buf.shape[0] - 1
        self.here = here
        self.partner = remote(src, buf.at[1 + c], send.at[0], recv.at[0], {"chan": 1 - c})
        self.low = [
            remote(src, buf.at[last], send.at[1 + k], recv.at[1], {"rows": z - 1, "chan": k}) for k in (0, 1)
        ]
        self.high = [
            remote(src, buf.at[0], send.at[1 + k], recv.at[2], {"rows": z + 1, "chan": k}) for k in (0, 1)
        ]

    def each(self, act):
        here = self.here

        @pl.when((here.c == 0) & here.up)
        def _():
            for copy in self.low:
                act(copy)

        @pl.when((here.c == 1) & here.down)
        def _():
            for copy in self.high:
                act(copy)

        act(self.partner)

    def start(self):
        self.each(lambda copy: copy.start())

    def wait_send(self):
        self.each(lambda copy: copy.wait_send())

    def wait_recv(self, when=True):
        here = self.here
        self.partner.wait_recv()

        @pl.when(here.down)
        def _():
            self.low[0].wait_recv()

        @pl.when(here.up)
        def _():
            self.high[0].wait_recv()


def normed(v, gain):
    return v * lax.rsqrt(jnp.mean(v * v, axis=-1, keepdims=True) + 1e-06) * gain


def silu(v):
    return 0.5 * v * (1.0 + jnp.tanh(0.5 * v))


def stored_shifts(x, dst, row, rows):
    n, ch = x.shape
    col = lax.broadcasted_iota(jnp.int32, (n, ch), 0)
    dst[row] = jnp.where(col == 0, 0.0, pltpu.roll(x, 1, 0)).astype(BF)
    dst[rows + row] = x.astype(BF)
    dst[2 * rows + row] = jnp.where(col == n - 1, 0.0, pltpu.roll(x, n - 1, 0)).astype(BF)


def dot(a, b):
    return jnp.dot(a, b, preferred_element_type=F32)


def dot_t(a, b):
    return lax.dot_general(a, b, (((1,), (1,)), ((), ())), preferred_element_type=F32)


def run_taps(tap, taps_t, taps_h, frames, own):
    for back in range(taps_t):
        split = min(back, frames)
        low, high = (split, frames) if own else (0, split)
        if low < high:
            lax.fori_loop(0, taps_h, lambda i, _: (tap(taps_t - 1 - back, i, low, high), 0)[1], 0)


def picker(rows, cols, hit):
    k = lax.broadcasted_iota(jnp.int32, (rows, cols), 0)
    n = lax.broadcasted_iota(jnp.int32, (rows, cols), 1)
    return jnp.where(hit(k, n), 1.0, 0.0).astype(BF)


def first_part(
    here, latent, cache, gain_mid, gain_attn, w_hbm, mine_out, attn_out,
    w, halo, prior, halfs, hs, hr, xs, xr, ps, pr, es, er, ls, wsem, begun, x3, acc,
):
    frames, rows, width, ch = latent.shape
    part = w.shape[-2]
    c, z = here.c, here.z
    fetch = pltpu.make_async_copy(w_hbm, w, wsem)
    fetch.start()
    to_up = remote(latent.at[:, 0], halo.at[1], hs.at[0], hr.at[0], {"rows": z - 1})
    to_down = remote(latent.at[:, rows - 1], halo.at[0], hs.at[1], hr.at[1], {"rows": z + 1})
    across = remote(latent.at[:, c], prior.at[1 + c], xs, xr, {"segment": here.s + 1})
    local = pltpu.make_async_copy(cache.at[:, c], prior.at[1 + c], ls)
    spread = Spread(here, prior.at[1 + c], prior, ps, pr)

    pl.when(here.has_next)(lambda: across.start())
    pl.when(here.up)(lambda: to_up.start())
    pl.when(here.down)(lambda: to_down.start())

    @pl.when(jnp.logical_not(here.has_prev))
    def _():
        local.start()
        local.wait()

    begun()
    gain = gain_mid[...].reshape(1, ch)

    def fill(slot, row, x, active):
        v = x.astype(F32)
        if active:
            v = silu(normed(v, gain))
        stored_shifts(v, x3.at[slot], row, rows + 2)

    for f in range(frames):
        for r in range(rows):
            fill(frames + f, 1 + r, latent[f, r], True)

    @pl.when(here.has_prev)
    def _():
        across.wait_recv()

    spread.start()
    for ok, copy, k in ((here.up, to_down, 0), (here.down, to_up, 1)):
        row = 0 if k == 0 else rows + 1

        @pl.when(ok)
        def _():
            copy.wait_recv()
            for f in range(frames):
                fill(frames + f, row, halo[k, f], True)

        @pl.when(jnp.logical_not(ok))
        def _():
            for f in range(frames):
                for k in range(3):
                    x3[frames + f, k * (rows + 2) + row] = jnp.zeros((width, ch), BF)

    pick = picker(ch, part, lambda k, n: k == n + c * part)
    acc[: frames * rows * width, :part] = dot(latent[...].reshape(-1, ch), pick)

    taps_t, taps_h = w.shape[:2]

    def tap(kt, kh, low, high):
        def plane(k):
            at = pl.ds(k * (rows + 2) + kh, rows)
            return x3[low + kt : high + kt, at].reshape((high - low) * rows * width, ch)

        acc[low * rows * width : high * rows * width, :part] += sum(dot_t(plane(k), w[kt, kh, k]) for k in range(3))

    fetch.wait()
    run_taps(tap, taps_t, taps_h, frames, True)
    spread.wait_recv()
    for row in range(rows + 2):
        inside = True if 0 < row <= rows else (here.up if row == 0 else here.down)
        known = jnp.logical_and(here.z >= 0, inside)
        for active in (False, True):
            origin = here.has_prev if active else jnp.logical_not(here.has_prev)

            @pl.when(known & origin)
            def _():
                for f in range(frames):
                    fill(f, row, prior[row, f], active)

        if row in (0, rows + 1):

            @pl.when(jnp.logical_not(inside))
            def _():
                for f in range(frames):
                    for k in range(3):
                        x3[f, k * (rows + 2) + row] = jnp.zeros((width, ch), BF)

    run_taps(tap, taps_t, taps_h, frames, False)
    result = acc[: frames * rows * width, :part].astype(BF).reshape(frames, rows, width, part)
    halfs[0] = jnp.where(c == 0, result[:, 1].astype(F32), result[:, 0].astype(F32)).astype(BF)
    swap = remote(halfs.at[0], halfs.at[1], es, er, {"chan": 1 - c})
    swap.start()
    kept = jnp.where(c == 0, result[:, 0].astype(F32), result[:, 1].astype(F32)).astype(BF)
    put = [picker(part, ch, lambda k, n: n == k + off * part) for off in (c, 1 - c)]
    full = dot(kept.reshape(-1, part), put[0])
    swap.wait()
    full = full + dot(halfs[1].reshape(-1, part), put[1])
    mine_out[...] = full.astype(BF).reshape(frames, width, ch)
    attn_out[...] = normed(full, gain_attn[...].reshape(1, ch)).astype(BF).reshape(frames, width, ch)
    spread.wait_send()
    pl.when(here.has_next)(lambda: across.wait_send())
    pl.when(here.up)(lambda: to_up.wait_send())
    pl.when(here.down)(lambda: to_down.wait_send())


def attn_part(here, later, mine, attn_in, wqkv, wproj, out, every, scores, values, query, send, recv):
    frames, width, ch = attn_in.shape
    z, c, chips = here.z, here.c, here.rows
    def copy(src, row, f, kind, target):
        return remote(src, every.at[row, f], send.at[row, f, kind], recv.at[row, f], target)

    links = ((0, here.down, {"rows": z + 1}), (1, here.up, {"rows": z - 1}))
    partner = {"chan": 1 - c}
    own = 2 * z + c
    for f in range(frames):
        for kind, ok, target in links:
            pl.when(ok)(lambda: copy(attn_in.at[f], own, f, kind, target).start())
        copy(attn_in.at[f], own, f, 2, partner).start()

    scale = 1.0 / math.sqrt(ch)

    def process(row, f, x):
        kv = dot(x, wqkv[:, ch:]).astype(BF)
        values[row, f] = kv[:, ch:]
        scores[row, f] = (
            lax.dot_general(query[f], kv[:, :ch], (((1,), (1,)), ((), ())), preferred_element_type=F32) * scale
        )

    for f in range(frames):
        query[f] = dot(attn_in[f], wqkv[:, :ch]).astype(BF)
        process(own, f, attn_in[f])

    def other(row, f):
        copy(attn_in.at[f], row, f, 2, partner).wait_recv()
        process(row, f, every[row, f])

    for f in range(frames):
        other(2 * z + 1 - c, f)
    later()

    def hop(k, _):
        sides = ((z - k, z - k >= 0, links[0]), (z + k, z + k < chips, links[1]))
        for f in range(frames):
            for src, valid, (kind, ok, target) in sides:
                row = 2 * src + c

                @pl.when(valid)
                def _():
                    copy(attn_in.at[f], row, f, kind, target).wait_recv()
                    copy(every.at[row, f], row, f, 2, partner).start()

                    @pl.when(ok)
                    def _():
                        copy(every.at[row, f], row, f, kind, target).start()

        for src, valid, _ in sides:

            @pl.when(valid)
            def _():
                for f in range(frames):
                    process(2 * src + c, f, every[2 * src + c, f])
                for f in range(frames):
                    other(2 * src + 1 - c, f)

        return 0

    lax.fori_loop(1, chips, hop, 0)

    for f in range(frames):
        part = scores[:, f]
        top = jnp.max(jnp.max(part, axis=0), axis=-1, keepdims=True)
        e = jnp.exp(part - top[None])
        total = jnp.sum(jnp.sum(e, axis=0), axis=-1, keepdims=True)
        weights = (e / total[None]).astype(BF)
        mixed = jnp.zeros((width, ch), F32)
        for row in range(2 * chips):
            mixed = mixed + dot(weights[row], values[row, f])
        out[f] = (mine[f].astype(F32) + dot(mixed.astype(BF), wproj[...])).astype(BF)

    for f in range(frames):
        for kind, ok, target in links:
            pl.when(ok)(lambda: copy(attn_in.at[f], own, f, kind, target).wait_send())
        copy(attn_in.at[f], own, f, 2, partner).wait_send()

    def drain(k, _):
        for f in range(frames):
            for src, valid, (kind, ok, target) in (
                (z - k, z - k >= 0, links[0]),
                (z + k, z + k < chips, links[1]),
            ):
                row = 2 * src + c

                @pl.when(valid)
                def _():
                    copy(every.at[row, f], row, f, 2, partner).wait_send()

                    @pl.when(ok)
                    def _():
                        copy(every.at[row, f], row, f, kind, target).wait_send()

        return 0

    lax.fori_loop(1, chips, drain, 0)


class Deal:
    def __init__(self, here, src, buf, send, recv):
        c, z, last = here.c, here.z, buf.shape[0] - 1
        self.here = here
        self.local = pltpu.make_async_copy(src.at[c], buf.at[1 + c], send.at[3])
        self.partner = remote(src.at[1 - c], buf.at[1 + c], send.at[0], recv.at[0], {"chan": 1 - c})
        self.low = [
            remote(src.at[k], buf.at[last], send.at[1 + k], recv.at[1], {"rows": z - 1, "chan": k}) for k in (0, 1)
        ]
        self.high = [
            remote(src.at[k], buf.at[0], send.at[1 + k], recv.at[2], {"rows": z + 1, "chan": k}) for k in (0, 1)
        ]

    def each(self, act):
        here = self.here

        @pl.when((here.c == 0) & here.up)
        def _():
            for copy in self.low:
                act(copy)

        @pl.when((here.c == 1) & here.down)
        def _():
            for copy in self.high:
                act(copy)

        act(self.partner)

    def start(self):
        self.each(lambda copy: copy.start())
        self.local.start()

    def wait_send(self):
        self.each(lambda copy: copy.wait_send())

    def wait_recv(self):
        here = self.here
        self.local.wait()
        self.partner.wait_recv()
        pl.when(here.down)(lambda: self.low[0].wait_recv())
        pl.when(here.up)(lambda: self.high[0].wait_recv())


def last_part(
    here, second, cache, gain, wup, wlow_hbm, out, x, acc,
    wlow, own, stage, prior, chalo, wfull, wmix, wtap, grid, upper,
    ss, sr, xs, xr, ps, pr, cs, cr, ws, wr, ls, fs, es, er, us, ur,
):
    frames, width, ch = second.shape
    c, z = here.c, here.z
    tall = cache.shape[1]
    low = cache.shape[2]
    wide = cache.shape[3]
    two = 2 * low
    part = wup.shape[2]
    first = jnp.logical_not(here.has_prev)
    fetch = pltpu.make_async_copy(wlow_hbm, wlow, fs)
    fetch.start()
    local = pltpu.make_async_copy(wup, wfull.at[c], ls)
    local.start()
    across = remote(second, stage, xs, xr, {"segment": here.s + 1})
    spread = Deal(here, second, own, ss, sr)
    relay = Deal(here, stage, prior, ps, pr)
    to_up = remote(cache.at[:, 0], chalo.at[1], cs.at[0], cr.at[0], {"rows": z - 1})
    to_down = remote(cache.at[:, tall - 1], chalo.at[0], cs.at[1], cr.at[1], {"rows": z + 1})
    weights = remote(wup, wfull.at[c], ws, wr, {"chan": 1 - c})

    weights.start()
    yield
    for edge, inside in ((0, here.up), (own.shape[0] - 1, here.down)):

        @pl.when(jnp.logical_not(inside))
        def _():
            own[edge] = jnp.zeros(own.shape[1:], BF)
            prior[edge] = jnp.zeros(own.shape[1:], BF)

    taps_t, taps_h = wlow.shape[:2]
    fetch.wait()

    def lay(i, _):
        kt, kh = i // taps_h, i % taps_h
        tap = [wlow[kt, kh, k * low : (k + 1) * low] for k in range(3)]
        none = jnp.zeros((low, part), BF)
        blocks = ((tap[1], tap[0]), (tap[2], tap[1]), (none, tap[2]), (tap[0], none))
        for at, (even, odd) in enumerate(blocks):
            wtap[kt, kh, at * low : (at + 1) * low, :] = jnp.concatenate([even, odd], axis=1)
        return 0

    lax.fori_loop(0, taps_t * taps_h, lay, 0)

    local.wait()
    weights.wait_recv()
    for kh in range(3):
        for at, sides in enumerate(((1, 1), (2, 0), (0, 2))):
            for side, kw in enumerate(sides):
                for half in (0, 1):
                    start = side * low + half * part
                    wmix[kh, at, start : start + part] = wfull[half, kh, kw]

    yield
    pl.when(here.has_next)(lambda: across.start())
    spread.start()
    pl.when(first & here.up)(lambda: to_up.start())
    pl.when(first & here.down)(lambda: to_down.start())
    spread.wait_recv()

    @pl.when(here.has_prev)
    def _():
        across.wait_recv()
        relay.start()

    gains = gain[...].reshape(1, low)
    gains = jnp.concatenate([gains, gains], axis=1)
    lane = lax.broadcasted_iota(jnp.int32, (width, two), 1)
    col = lax.broadcasted_iota(jnp.int32, (width, two), 0)
    evens = lane < low

    def spaced(v, keep_first, keep_last):
        v_next = jnp.where(col == width - 1, 0.0, pltpu.roll(v, width - 1, 0))
        v_prev = jnp.where(col == 0, 0.0, pltpu.roll(v, 1, 0))
        return jnp.where(evens, keep_first(v_prev, v_next), keep_last(v_prev, v_next))

    def beside(slot, row, v):
        x[slot, tall + 2 + row] = spaced(v, lambda p, n: n, lambda p, n: p).astype(BF)

    def put(slot, row, v):
        x[slot, row] = v.astype(BF)
        beside(slot, row, v)

    height = own.shape[0]

    def row_copy(slot, at, r):
        piece = x.at[slot, r]
        return remote(piece, piece, es.at[at, r], er.at[at, r], {"chan": 1 - c})

    def upper_copy(f, r):
        return remote(upper.at[f, r], upper.at[f, r], us.at[r], ur.at[r], {"chan": 1 - c})

    def raise_frame(tile, at):
        slot = at * frames + c
        for kh in range(3):
            n0, n1 = (0, height - 1) if kh == 0 else (0, height) if kh == 1 else (1, height)
            flat = tile[n0:n1].reshape((n1 - n0) * width, ch)
            g0 = sum((height - 1, height)[:kh])
            g1 = g0 + n1 - n0
            grid[g0:g1, :, :two] = (dot_t(flat, wmix[kh, 0]) + dot_t(flat, wmix[kh, 1])).reshape(
                n1 - n0, width, two
            )
            grid[g0:g1, :, two:] = dot_t(flat, wmix[kh, 2]).reshape(n1 - n0, width, two)
        for r in range(tall + 2):
            i, odd = (r + 1) // 2, (r + 1) % 2
            sources = (i, i, i + 1) if odd else (i - 1, i, i)
            both = grid[sources[0]] + grid[height - 1 + sources[1]] + grid[2 * height - 2 + sources[2]]
            v = both[:, :two] + spaced(both[:, two:], lambda p, n: p, lambda p, n: n)
            v = v.astype(BF)
            if at and 0 < r <= tall:
                upper[c, r - 1] = v
                upper_copy(c, r - 1).start()
            v = v.astype(F32)
            sq = v * v
            mean_even = jnp.sum(jnp.where(evens, sq, 0.0), axis=-1, keepdims=True) / low
            mean_odd = jnp.sum(jnp.where(evens, 0.0, sq), axis=-1, keepdims=True) / low
            v = v * jnp.where(evens, lax.rsqrt(mean_even + 1e-06), lax.rsqrt(mean_odd + 1e-06)) * gains
            v = silu(v)
            if r == 0:
                v = jnp.where(here.up, v, 0.0)
            if r == tall + 1:
                v = jnp.where(here.down, v, 0.0)
            put(slot, r, v)
            row_copy(slot, at, r).start()
        other = at * frames + 1 - c
        for r in range(tall + 2):
            row_copy(other, at, r).wait_recv()
            beside(other, r, x[other, r].astype(F32))

    raise_frame(own, 1)
    acc[...] = jnp.zeros(acc.shape, F32)

    def tap(kt, kh, low, high):
        def plane(k):
            at = pl.ds(k * (tall + 2) + kh, tall)
            return x[low + kt : high + kt, at].reshape((high - low) * tall * width, two)

        v = jnp.concatenate([plane(0), plane(1)], axis=1)
        acc[low * tall * width : high * tall * width] += dot(v, wtap[kt, kh])

    run_taps(tap, taps_t, taps_h, frames, True)

    @pl.when(here.has_prev)
    def _():
        relay.wait_recv()
        raise_frame(prior, 0)

    spots = [picker(width, wide, lambda k, n: n == 2 * k + p) for p in (0, 1)]

    def take(slot, row, flipped):
        put(slot, row, jnp.concatenate([dot_t(spot, flipped) for spot in spots], axis=1))

    @pl.when(first)
    def _():
        def each(i, _):
            take(i // tall, 1 + i % tall, cache[i // tall, i % tall])
            return 0

        lax.fori_loop(0, frames * tall, each, 0)

    for row, inside, k, copy in ((0, here.up, 0, to_down), (tall + 1, here.down, 1, to_up)):

        @pl.when(first & inside)
        def _():
            copy.wait_recv()
            for f in range(frames):
                take(f, row, chalo[k, f])

        @pl.when(first & jnp.logical_not(inside))
        def _():
            for f in range(frames):
                put(f, row, jnp.zeros((width, two), F32))

    run_taps(tap, taps_t, taps_h, frames, False)
    n = 2 * part
    pick = picker(two, n, lambda k, j: k == jnp.where(j < part, j, j - part + low) + c * part)
    for r in range(tall):
        upper_copy(1 - c, r).wait_recv()
    acc[...] += dot(upper[...].reshape(-1, two), pick)

    def finish(i, _):
        done = acc[pl.ds(pl.multiple_of(i * width, width), width), :].T.astype(BF)
        out[i // tall, i % tall] = (dot(done[:part], spots[0]) + dot(done[part:], spots[1])).astype(BF)
        return 0

    lax.fori_loop(0, frames * tall, finish, 0)
    spread.wait_send()
    weights.wait_send()
    for r in range(tall):
        upper_copy(c, r).wait_send()
    for r in range(tall + 2):
        row_copy(frames + c, 1, r).wait_send()

    @pl.when(here.has_prev)
    def _():
        relay.wait_send()
        for r in range(tall + 2):
            row_copy(c, 0, r).wait_send()

    pl.when(here.has_next)(lambda: across.wait_send())
    pl.when(first & here.up)(lambda: to_up.wait_send())
    pl.when(first & here.down)(lambda: to_down.wait_send())


def whole_kernel(counts, *refs):
    groups = []
    for count in counts:
        groups.append(refs[:count])
        refs = refs[count:]
    ins, (out,), shared, first, attn, last = groups
    latent, cache_mid, cache_low, gain_mid, gain_attn, gain_low, conv_mid, attn_qkv, attn_proj, conv_up, conv_low = ins
    mine, attn_in, second, wqkv, wproj, low_cache, sems, x, acc = shared
    fetches = [
        pltpu.make_async_copy(src, dst, sems.at[i])
        for i, (src, dst) in enumerate(((attn_qkv, wqkv), (attn_proj, wproj), (cache_low, low_cache)))
    ]
    here = Place()
    here.greet(True, True)
    tail = last_part(here, second, low_cache, gain_low, conv_up, conv_low, out, x, acc, *last)
    first_part(here, latent, cache_mid, gain_mid, gain_attn, conv_mid, mine, attn_in, *first, lambda: start(tail, fetches), x, acc)
    for fetch in fetches:
        fetch.wait()
    attn_part(here, lambda: next(tail), mine, attn_in, wqkv, wproj, second, *attn)
    next(tail, None)


def start(tail, fetches):
    for fetch in fetches:
        fetch.start()
    next(tail)


def call(kernel, number, outs, scratch, *args, far=()):
    return pl.pallas_call(
        kernel,
        out_shape=outs,
        in_specs=[pl.BlockSpec(memory_space=pl.ANY if i in far else pltpu.VMEM) for i in range(len(args))],
        out_specs=jax.tree.map(lambda _: pl.BlockSpec(memory_space=pltpu.VMEM), outs),
        scratch_shapes=scratch,
        compiler_params=pltpu.CompilerParams(
            collective_id=number, has_side_effects=True, vmem_limit_bytes=67043328
        ),
    )(*args)


def body(
    latent, cache_mid, cache_low, gain_mid, gain_attn, gain_low, conv_mid, attn_qkv, attn_proj, conv_up, conv_low
):
    frames, rows, width, ch = latent.shape
    part = conv_mid.shape[-1]
    dma, one = pltpu.SemaphoreType.DMA, pltpu.SemaphoreType.DMA(())
    row = jax.ShapeDtypeStruct((frames, width, ch), BF)
    taps_t, taps_h, taps_w = conv_mid.shape[:3]
    total = rows * lax.axis_size("rows")
    vm = pltpu.VMEM(row.shape, BF)
    cache_t = jnp.swapaxes(cache_low, 2, 3)
    shared = [
        vm, vm, vm, pltpu.VMEM(attn_qkv.shape, BF), pltpu.VMEM(attn_proj.shape, BF), pltpu.VMEM(cache_t.shape, BF),
        dma((3,)),
        pltpu.VMEM((2 * frames, max(taps_w * (rows + 2), 2 * (cache_low.shape[1] + 2)), width, ch), BF),
        pltpu.VMEM((frames * cache_low.shape[1] * width, 2 * conv_low.shape[-1]), F32),
    ]
    first = [
            pltpu.VMEM((taps_t, taps_h, taps_w, part, ch), BF),
            pltpu.VMEM((2, frames, width, ch), BF),
            pltpu.VMEM((rows + 2, frames, width, ch), BF),
            pltpu.VMEM((2, frames, width, part), BF),
            dma((2,)), dma((2,)), one, one, dma((3,)), dma((3,)), one, one, one, one,
    ]
    attn = [
            pltpu.VMEM((total, frames, width, ch), BF),
            pltpu.VMEM((total, frames, width, width), F32),
            pltpu.VMEM((total, frames, width, ch), BF),
            pltpu.VMEM((frames, width, ch), BF),
            dma((total, frames, 3)),
            dma((total, frames)),
    ]
    _, tall, wide, low = cache_low.shape
    cut = conv_low.shape[-1]
    two = 2 * low
    taps_t, taps_h, taps_w = conv_low.shape[:3]
    last = [
            pltpu.VMEM((taps_t, taps_h, taps_w * low, cut), BF),
            pltpu.VMEM((rows + 2, width, ch), BF),
            pltpu.VMEM((frames, width, ch), BF),
            pltpu.VMEM((rows + 2, width, ch), BF),
            pltpu.VMEM((2, frames, low, wide), BF),
            pltpu.VMEM((2, 3, 3, cut, ch), BF),
            pltpu.VMEM((3, 3, two, ch), BF),
            pltpu.VMEM((taps_t, taps_h, 2 * two, 2 * cut), BF),
            pltpu.VMEM((3 * rows + 4, width, 2 * two), F32),
            pltpu.VMEM((frames, tall, width, two), BF),
            dma((4,)), dma((3,)), one, one, dma((4,)), dma((3,)), dma((2,)), dma((2,)), one, one, one, one,
            dma((2, tall + 2)), dma((2, tall + 2)), dma((tall,)), dma((tall,)),
    ]
    args = (
        latent, cache_mid, cache_t, gain_mid, gain_attn, gain_low, jnp.swapaxes(conv_mid, 3, 4), attn_qkv, attn_proj,
        jnp.swapaxes(conv_up, 2, 3), conv_low.reshape(taps_t, taps_h, taps_w * low, cut),
    )
    counts = (len(args), 1, len(shared), len(first), len(attn), len(last))
    decoded = call(
        functools.partial(whole_kernel, counts),
        0,
        jax.ShapeDtypeStruct((frames, tall, cut, wide), BF),
        shared + first + attn + last,
        *args,
        far=(2, 6, 7, 8, 10),
    )
    return jnp.swapaxes(decoded, 2, 3)


def solution(mesh):
    placed = (
        P(("groups", "segment"), "rows", None, None),
        P("groups", "rows", None, None),
        P("groups", "rows", None, None),
        P(),
        P(),
        P(),
        P(None, None, None, None, "chan"),
        P(),
        P(),
        P(None, None, None, "chan"),
        P(None, None, None, None, "chan"),
    )
    return jax.shard_map(
        body,
        mesh=mesh,
        in_specs=placed,
        out_specs=P(("groups", "segment"), "rows", None, "chan"),
        check_vma=False,
    )
```
